32 devices in a mesh: groups: 2 (over x), ty: 4 (over y, core), tx: 4 (over z).
Axes of the slice: x: 2, y: 2, z: 4, core: 2. Of those that a mesh axis runs over, the one named last changes fastest.
Arguments:
- object_planes: float32 [4, 2048, 1024], P(None, ('groups', 'ty'), 'tx'), parts along dimension 1, may hold values from -5 to 5
- probe: float32 [2, 256, 256], replicated, may hold values from -5 to 5
- phase: float32 [256, 256], replicated, may hold values from -3.140625 to 3.140625
- coords: int32 [8, 4, 4, 2], P(('groups', 'ty'), 'tx'), parts along dimension 0, may hold values from 0 to 255
- live: int32 [8, 4], P(('groups', 'ty'), 'tx'), parts along dimension 0, may hold values from 0 to 4, as said below
- amplitude: float32 [8, 4, 4, 256, 256], P(('groups', 'ty'), 'tx'), parts along dimension 0, may hold values from 0 to 2
Outputs:
- updated: float32 [4, 2048, 1024], P(None, ('groups', 'ty'), 'tx'), parts along dimension 1
The draws below stay inside these ranges and needn't reach their ends.
There are 2 independent parts, one for each index of `groups`. The reference program is written for one: setup_inputs(seed, part) draws one part's arguments, and reference() takes and returns one part's arrays. A program takes and returns all parts, laid end to end along the dimension named above; an argument that names none is the same for every part. Nothing has to cross between parts.
Inputs may be any that keep to these rules, and one draw needn't show every extreme that they name: Only slots below live of their tile are used; some tile holds 4 live slots.
All inputs are finite; a program needn't handle non-finite values.
Results may differ from the reference program's by a relative error of at most 0.0003.
Values sent between devices are 32-bit elements; how exact they have to be, the bound alone decides.
A program may use at most 128 MiB of HBM per device.

```python
import math
import jax
import jax.numpy as jnp
from jax import lax

W = 256
SLOTS = 4
TILES_Y = 4
TILES_X = 4
NH = 1024
NW = 1024


def draw_live(key, part):
    key_base, key_cols, key_start = jax.random.split(key, 3)
    base_load = jax.random.randint(key_base, (TILES_Y, TILES_X), 0, 3)
    dense_cols = jax.random.randint(key_cols, (2,), 0, TILES_X)
    start_row = jax.random.randint(key_start, (), 0, TILES_Y)
    row_hit = (jnp.arange(TILES_Y) - start_row) % TILES_Y < max(TILES_Y // 4, 1)
    col_hit = jnp.any(jnp.arange(TILES_X)[None, :] == dense_cols[:, None], axis=0)
    dense = row_hit[:, None] & col_hit[None, :]
    return jnp.where(dense, SLOTS, base_load).astype(jnp.int32)


def touch_ends(array, key, smallest, high):
    longest = array.shape.index(max(array.shape))
    spots = []
    for shift in (0, 1):
        where = [jax.random.randint(jax.random.fold_in(key, axis), (), 0, length) for axis, length in enumerate(array.shape)]
        where[longest] = (where[longest] + shift) % array.shape[longest]
        spots.append(tuple(where))
    return array.at[spots[0]].set(smallest).at[spots[1]].set(high)


def level_of(key, dims, shards, smallest, top_value):
    def one(axis_at, blocks):
        draws = jax.random.uniform(jax.random.fold_in(jax.random.fold_in(key, 6), axis_at), (blocks,), jnp.float32, smallest / len(shards), top_value / len(shards))
        return jnp.repeat(jnp.exp(draws), dims[axis_at] // blocks).reshape((-1,) + (1,) * (len(dims) - axis_at - 1))

    gain = one(*shards[0])
    for cut in shards[1:]:
        gain = gain * one(*cut)
    return gain


def noise(rng, shape, deviation, bound, pieces=(), kind=jnp.bfloat16):
    loudness = level_of(rng, shape, pieces, -0.22, 0.18) if pieces else 1.0
    values = jax.random.normal(rng, shape, jnp.float32) * deviation * loudness
    return jnp.minimum(jnp.maximum(values, -bound), bound).astype(kind)


def setup_inputs(seed: int = 0, part: int = 0) -> dict:
    seeds = jax.random.split(jax.random.key(seed), 7)
    part_keys = jax.random.split(jax.random.fold_in(seeds[6], part), 7)
    return {
        "object_planes": noise(part_keys[0], (4, NH, NW), 0.7, 5.0, ((1, 4), (2, 4)), jnp.float32),
        "probe": noise(seeds[1], (2, W, W), 0.7, 5.0, (), jnp.float32),
        "phase": jnp.clip(jax.random.uniform(seeds[2], (W, W), jnp.float32, -3.140625, 3.140625), -3.140625, 3.140625),
        "coords": touch_ends(jax.random.randint(part_keys[3], (TILES_Y, TILES_X, SLOTS, 2), 0, W), jax.random.fold_in(part_keys[3], 1), 0, W - 1).astype(jnp.int32),
        "live": draw_live(jax.random.fold_in(jax.random.fold_in(seeds[6], part), 71), part),
        "amplitude": jnp.clip(2.0 * jax.random.uniform(part_keys[5], (TILES_Y, TILES_X, SLOTS, W, W), jnp.float32) ** level_of(part_keys[5], (TILES_Y, TILES_X, SLOTS, W, W), ((0, 4), (1, 4)), -0.2, 0.2), 0.0, 2.0),
    }


HIGH = lax.Precision.HIGHEST

def dft_tables(probe_width):
    index_grid = jnp.arange(probe_width, dtype=jnp.int32)[:, None] * jnp.arange(probe_width, dtype=jnp.int32)[None, :] % probe_width
    angles = index_grid.astype(jnp.float32) * (2.0 * math.pi / probe_width)
    norm_scale = 1.0 / math.sqrt(probe_width)
    return (jnp.cos(angles) * norm_scale, -jnp.sin(angles) * norm_scale)

def product(left_mat, right_mat):
    return jnp.dot(left_mat, right_mat, precision=HIGH, preferred_element_type=jnp.float32)

def transform(real_part, imag_part, cos_table, sin_table):
    left_r = product(cos_table, real_part) - product(sin_table, imag_part)
    left_i = product(cos_table, imag_part) + product(sin_table, real_part)
    out_r = product(left_r, cos_table) - product(left_i, sin_table)
    out_i = product(left_r, sin_table) + product(left_i, cos_table)
    return (out_r, out_i)

def slot_terms(probe, phase_r, phase_i, cos_table, sin_table, patch, amp_plane):
    probe_r, probe_i = (probe[0], probe[1])
    first_r, first_i, second_r, second_i = (patch[0], patch[1], patch[2], patch[3])
    wave_one_r = probe_r * first_r - probe_i * first_i
    wave_one_i = probe_r * first_i + probe_i * first_r
    spec_r, spec_i = transform(wave_one_r, wave_one_i, cos_table, sin_table)
    moved_r = spec_r * phase_r - spec_i * phase_i
    moved_i = spec_r * phase_i + spec_i * phase_r
    wave_two_r, wave_two_i = transform(moved_r, moved_i, cos_table, -sin_table)
    exit_r = wave_two_r * second_r - wave_two_i * second_i
    exit_i = wave_two_r * second_i + wave_two_i * second_r
    far_r, far_i = transform(exit_r, exit_i, cos_table, sin_table)
    ratio = amp_plane / jnp.maximum(jnp.sqrt(far_r * far_r + far_i * far_i), 0.5) - 1.0
    back_r, back_i = transform(far_r * ratio, far_i * ratio, cos_table, -sin_table)
    grad_two_r = wave_two_r * back_r + wave_two_i * back_i
    grad_two_i = wave_two_r * back_i - wave_two_i * back_r
    inner_r = second_r * back_r + second_i * back_i
    inner_i = second_r * back_i - second_i * back_r
    turn_r, turn_i = transform(inner_r, inner_i, cos_table, sin_table)
    undo_r = turn_r * phase_r + turn_i * phase_i
    undo_i = turn_i * phase_r - turn_r * phase_i
    prior_r, prior_i = transform(undo_r, undo_i, cos_table, -sin_table)
    grad_one_r = probe_r * prior_r + probe_i * prior_i
    grad_one_i = probe_r * prior_i - probe_i * prior_r
    power_two = wave_two_r * wave_two_r + wave_two_i * wave_two_i
    return jnp.stack([grad_one_r, grad_one_i, grad_two_r, grad_two_i, power_two])

def reference(object_planes, probe, phase, coords, live, amplitude):
    probe_width = probe.shape[-1]
    cos_table, sin_table = dft_tables(probe_width)
    phase_r, phase_i = (jnp.cos(phase), jnp.sin(phase))
    padded = jnp.pad(object_planes, ((0, 0), (0, probe_width), (0, probe_width)))
    totals = jnp.zeros((6,) + padded.shape[1:], jnp.float32)
    probe_power = probe[0] * probe[0] + probe[1] * probe[1]
    tiles_rows, tiles_cols, slot_count = (coords.shape[0], coords.shape[1], coords.shape[2])
    flat_coords = coords.reshape(-1, 2)
    flat_amp = amplitude.reshape(-1, probe_width, probe_width)
    tile_row = jnp.repeat(jnp.arange(tiles_rows, dtype=jnp.int32), tiles_cols * slot_count)
    tile_col = jnp.tile(jnp.repeat(jnp.arange(tiles_cols, dtype=jnp.int32), slot_count), tiles_rows)
    slot_ids = jnp.tile(jnp.arange(slot_count, dtype=jnp.int32), tiles_rows * tiles_cols)
    active = slot_ids < live.reshape(-1)[tile_row * tiles_cols + tile_col]

    def accumulate(totals, slot_data):
        where_yx, amp_plane, row_tile, col_tile, is_live = slot_data
        top_row = (row_tile * probe_width + where_yx[0]).astype(jnp.int32)
        left_col = (col_tile * probe_width + where_yx[1]).astype(jnp.int32)
        zero_index = jnp.int32(0)
        patch = lax.dynamic_slice(padded, (zero_index, top_row, left_col), (4, probe_width, probe_width))

        def compute():
            gradients = slot_terms(probe, phase_r, phase_i, cos_table, sin_table, patch, amp_plane)
            return jnp.concatenate([gradients[0:2], probe_power[None], gradients[2:5]])

        def skip():
            return jnp.zeros((6, probe_width, probe_width), jnp.float32)
        contrib = lax.cond(is_live, compute, skip)
        current = lax.dynamic_slice(totals, (zero_index, top_row, left_col), (6, probe_width, probe_width))
        return (lax.dynamic_update_slice(totals, current + contrib, (zero_index, top_row, left_col)), None)
    totals, _ = lax.scan(accumulate, totals, (flat_coords, flat_amp, tile_row, tile_col, active))
    totals = totals[:, :object_planes.shape[1], :object_planes.shape[2]]
    first = object_planes[0:2] + totals[0:2] / (totals[2:3] + 1.0)
    second = object_planes[2:4] + totals[3:5] / (totals[5:6] + 1.0)
    return jnp.concatenate([first, second])
```

```python
import math

import jax
import jax.numpy as jnp
import numpy as np
from jax import lax
from jax.experimental import pallas as pl
from jax.experimental.pallas import tpu as pltpu
from jax.sharding import PartitionSpec as P

F32 = jnp.float32
BF16 = jnp.bfloat16


def from_behind(block, axis, distance):
    devices = range(lax.axis_size(axis))
    route = [(i - distance, i) for i in devices if i - distance in devices]
    return lax.ppermute(block, axis, route)


def split_tables(width):
    index = np.arange(width)[:, None] * np.arange(width)[None, :] % width
    angles = index * (2.0 * math.pi / width)
    scale = 1.0 / math.sqrt(width)
    cos_table = (np.cos(angles) * scale).astype(np.float32)
    sin_table = (-np.sin(angles) * scale).astype(np.float32)

    def parts(table):
        high = table.astype(BF16)
        low = (table - high.astype(np.float32)).astype(BF16)
        return high, high, low

    left = np.concatenate(
        [
            np.concatenate([*parts(cos_table), *parts(-sin_table)], axis=1),
            np.concatenate([*parts(sin_table), *parts(cos_table)], axis=1),
        ],
        axis=0,
    )
    return jnp.asarray(left), jnp.asarray(np.ascontiguousarray(left.T))


def split(value):
    high = value.astype(BF16)
    low = (value - high.astype(F32)).astype(BF16)
    return high, low


def forward(parts_r, parts_i, left_ref, right_ref):
    width = parts_r[0].shape[0]
    columns = []
    for real, imag in zip(parts_r, parts_i):
        high_r, low_r = split(real)
        high_i, low_i = split(imag)
        columns.append(jnp.concatenate([high_r, low_r, high_r, high_i, low_i, high_i], axis=0))
    data = jnp.concatenate(columns, axis=1)
    half = jnp.dot(left_ref[...], data, preferred_element_type=F32)
    rows = []
    for at in range(len(parts_r)):
        cut = slice(at * width, (at + 1) * width)
        high_r, low_r = split(half[:width, cut])
        high_i, low_i = split(half[width:, cut])
        rows.append(jnp.concatenate([high_r, low_r, high_r, high_i, low_i, high_i], axis=1))
    data = jnp.concatenate(rows, axis=0)
    whole = jnp.dot(data, right_ref[...], preferred_element_type=F32)
    out_r = [whole[at * width : (at + 1) * width, :width] for at in range(len(parts_r))]
    out_i = [whole[at * width : (at + 1) * width, width:] for at in range(len(parts_r))]
    return out_r, out_i


def fill_region(region, own, right, down, diag):
    width = own.shape[-1]
    region[:, :width, :width] = own[...]
    region[:, :width, width:] = right[...]
    region[:, width:, :width] = down[...]
    region[:, width:, width:] = diag[...]


def window(region, plane, top, left):
    width = region.shape[-1] // 2
    base = pl.multiple_of(top // 8 * 8, 8)
    extra = top - base
    rows = region[plane, pl.ds(base, width + 8), :]
    back = jnp.where(left == 0, 0, 2 * width - left)
    rows = pltpu.roll(rows, back, 1)[:, :width]
    up = jnp.where(extra == 0, 0, width + 8 - extra)
    return pltpu.roll(rows, up, 0)[:width]


def deposit(totals, plane, value, top, left):
    width = value.shape[0]
    base = pl.multiple_of(top // 8 * 8, 8)
    tall = jnp.concatenate([value, jnp.zeros((8, width), F32)], axis=0)
    tall = pltpu.roll(tall, top - base, 0)
    wide = pltpu.roll(jnp.concatenate([tall, jnp.zeros_like(tall)], axis=1), left, 1)
    totals[plane, pl.ds(base, width + 8), :] += wide


def write_quarters(totals, upper_left, upper_right, lower_left, lower_right):
    width = upper_left.shape[-1]
    upper_left[...] = totals[:, :width, :width]
    upper_right[...] = totals[:, :width, width:]
    lower_left[...] = totals[:, width:, :width]
    lower_right[...] = totals[:, width:, width:]


def norm_kernel(coords, live, probe, *refs):
    *quarters, totals = refs
    totals[...] = jnp.zeros_like(totals)

    @pl.loop(0, live[0])
    def _(slot):
        power = probe[0] * probe[0] + probe[1] * probe[1]
        deposit(totals, 0, power, coords[slot, 0], coords[slot, 1])

    write_quarters(totals, *quarters)


def wave_kernel(group, coords, own, right, down, diag, probe, phase, left_t, right_t, wave, region):
    fill_region(region, own, right, down, diag)

    @pl.loop(0, coords.shape[0] // group)
    def _(step):
        in_r, in_i = [], []
        for at in range(group):
            slot = step * group + at
            top, left = coords[slot, 0], coords[slot, 1]
            first_r, first_i = window(region, 0, top, left), window(region, 1, top, left)
            in_r.append(probe[0] * first_r - probe[1] * first_i)
            in_i.append(probe[0] * first_i + probe[1] * first_r)
        spec_r, spec_i = forward(in_r, in_i, left_t, right_t)
        moved_r = [a * phase[0] - b * phase[1] for a, b in zip(spec_r, spec_i)]
        minus_i = [-(a * phase[1] + b * phase[0]) for a, b in zip(spec_r, spec_i)]
        wave_r, wave_i = forward(moved_r, minus_i, left_t, right_t)
        for at in range(group):
            wave[step * group + at, 0] = wave_r[at]
            wave[step * group + at, 1] = -wave_i[at]


def back_kernel(
    group, coords, live, wave, own, right, down, diag, amplitude, left_t, right_t, inner, *refs
):
    *quarters, region, totals = refs
    fill_region(region, own, right, down, diag)
    totals[...] = jnp.zeros_like(totals)

    @pl.loop(0, coords.shape[0] // group)
    def _(step):
        in_r, in_i = [], []
        for at in range(group):
            slot = step * group + at
            top, left = coords[slot, 0], coords[slot, 1]
            second_r, second_i = window(region, 0, top, left), window(region, 1, top, left)
            inner[slot, 0] = second_r
            inner[slot, 1] = second_i
            wave_r, wave_i = wave[slot, 0], wave[slot, 1]
            in_r.append(wave_r * second_r - wave_i * second_i)
            in_i.append(wave_r * second_i + wave_i * second_r)
        far_r, far_i = forward(in_r, in_i, left_t, right_t)
        ratio = [
            amplitude[step * group + at]
            * jnp.minimum(lax.rsqrt(far_r[at] * far_r[at] + far_i[at] * far_i[at]), 2.0)
            - 1.0
            for at in range(group)
        ]
        back_r, minus_i = forward(
            [a * b for a, b in zip(far_r, ratio)],
            [-a * b for a, b in zip(far_i, ratio)],
            left_t,
            right_t,
        )
        for at in range(group):
            slot = step * group + at
            top, left = coords[slot, 0], coords[slot, 1]
            real, imag = back_r[at], -minus_i[at]
            second_r, second_i = inner[slot, 0], inner[slot, 1]
            inner[slot, 0] = second_r * real + second_i * imag
            inner[slot, 1] = second_r * imag - second_i * real

            @pl.when(slot < live[0])
            def _():
                wave_r, wave_i = wave[slot, 0], wave[slot, 1]
                deposit(totals, 0, wave_r * real + wave_i * imag, top, left)
                deposit(totals, 1, wave_r * imag - wave_i * real, top, left)
                deposit(totals, 2, wave_r * wave_r + wave_i * wave_i, top, left)

    write_quarters(totals, *quarters)


def grad_kernel(group, coords, live, inner, probe, phase, left_t, right_t, *refs):
    *quarters, totals = refs
    totals[...] = jnp.zeros_like(totals)

    @pl.loop(0, coords.shape[0] // group)
    def _(step):
        in_r = [inner[step * group + at, 0] for at in range(group)]
        in_i = [inner[step * group + at, 1] for at in range(group)]
        turn_r, turn_i = forward(in_r, in_i, left_t, right_t)
        undo_r = [a * phase[0] + b * phase[1] for a, b in zip(turn_r, turn_i)]
        minus_i = [a * phase[1] - b * phase[0] for a, b in zip(turn_r, turn_i)]
        prior_r, minus_p = forward(undo_r, minus_i, left_t, right_t)
        for at in range(group):
            slot = step * group + at
            top, left = coords[slot, 0], coords[slot, 1]
            real, imag = prior_r[at], -minus_p[at]

            @pl.when(slot < live[0])
            def _():
                deposit(totals, 0, probe[0] * real + probe[1] * imag, top, left)
                deposit(totals, 1, probe[0] * imag - probe[1] * real, top, left)

    write_quarters(totals, *quarters)


def settle(quarters):
    upper_left, upper_right, lower_left, lower_right = quarters
    upper_right = upper_right + from_behind(lower_right, "ty", 1)
    from_above = from_behind(lower_left, "ty", 1)
    from_left = from_behind(upper_right, "tx", 1)
    return upper_left + from_above + from_left


def on_device(object_planes, probe, phase, coords, live, amplitude):
    width = probe.shape[-1]
    slots = coords.shape[2]
    group = 2 if slots % 2 == 0 else 1
    left_t, right_t = split_tables(width)
    phase_ri = jnp.stack([jnp.cos(phase), jnp.sin(phase)])
    where_yx = coords[0, 0]
    count = live[0]
    smem = pl.BlockSpec(memory_space=pltpu.SMEM)
    vmem = pl.BlockSpec(memory_space=pltpu.VMEM)

    def plane(*lead):
        return jax.ShapeDtypeStruct((*lead, width, width), F32)

    def scratch(planes):
        return pltpu.VMEM((planes, 2 * width, 2 * width), F32)

    dots = 2 * slots * 2 * 2 * width * 2 * width * 6 * width

    def call(body, n_smem, n_vmem, outs, scratches, flops, name):
        return pl.pallas_call(
            body,
            out_shape=outs,
            in_specs=[smem] * n_smem + [vmem] * n_vmem,
            out_specs=jax.tree.map(lambda _: vmem, outs),
            scratch_shapes=scratches,
            compiler_params=pltpu.CompilerParams(vmem_limit_bytes=48 << 20),
            cost_estimate=pl.CostEstimate(
                flops=flops, bytes_accessed=8 << 20, transcendentals=0
            ),
            name=name,
        )

    def quads(tile):
        right = from_behind(tile, "tx", -1)
        down = from_behind(tile, "ty", -1)
        return tile, right, down, from_behind(right, "ty", -1)

    first, second = object_planes[0:2], object_planes[2:4]
    first_quads = quads(first)
    second_quads = quads(second)

    norm = call(norm_kernel, 2, 1, [plane(1)] * 4, [scratch(1)], 1 << 20, "norm")(
        where_yx, count, probe
    )
    norm_sum = settle(norm)

    def bind(body):
        def bound(*refs):
            body(group, *refs)

        return bound

    wave = call(bind(wave_kernel), 1, 8, plane(slots, 2), [scratch(2)], dots, "wave")(
        where_yx, *first_quads, probe, phase_ri, left_t, right_t
    )
    inner, *second_sums = call(
        bind(back_kernel),
        2,
        8,
        [plane(slots, 2)] + [plane(3)] * 4,
        [scratch(2), scratch(3)],
        dots,
        "back",
    )(where_yx, count, wave, *second_quads, amplitude[0, 0], left_t, right_t)
    first_sums = call(bind(grad_kernel), 2, 5, [plane(2)] * 4, [scratch(2)], dots, "grad")(
        where_yx, count, inner, probe, phase_ri, left_t, right_t
    )
    second_sum = settle(second_sums)
    first_sum = settle(first_sums)
    new_first = first + first_sum / (norm_sum + 1.0)
    new_second = second + second_sum[0:2] / (second_sum[2:3] + 1.0)
    return jnp.concatenate([new_first, new_second])


def solution(mesh):
    return jax.shard_map(
        on_device,
        mesh=mesh,
        in_specs=(
            P(None, ("groups", "ty"), "tx"),
            P(),
            P(),
            P(("groups", "ty"), "tx", None, None),
            P(("groups", "ty"), "tx"),
            P(("groups", "ty"), "tx", None, None, None),
        ),
        out_specs=P(None, ("groups", "ty"), "tx"),
        check_vma=False,
    )
```

```python
import math

import jax
import jax.numpy as jnp
import numpy as np
from jax import lax
from jax.experimental import pallas as pl
from jax.experimental.pallas import tpu as pltpu
from jax.sharding import PartitionSpec as P

F32 = jnp.float32
BF16 = jnp.bfloat16


def split_tables(width):
    index = np.arange(width)[:, None] * np.arange(width)[None, :] % width
    angles = index * (2.0 * math.pi / width)
    scale = 1.0 / math.sqrt(width)
    cos_table = (np.cos(angles) * scale).astype(np.float32)
    sin_table = (-np.sin(angles) * scale).astype(np.float32)

    def parts(table):
        high = table.astype(BF16)
        low = (table - high.astype(np.float32)).astype(BF16)
        return high, high, low

    left = np.concatenate(
        [
            np.concatenate([*parts(cos_table), *parts(-sin_table)], axis=1),
            np.concatenate([*parts(sin_table), *parts(cos_table)], axis=1),
        ],
        axis=0,
    )
    return jnp.asarray(left), jnp.asarray(np.ascontiguousarray(left.T))


def split(value):
    high = value.astype(BF16)
    low = (value - high.astype(F32)).astype(BF16)
    return high, low


def forward(parts_r, parts_i, left_ref, right_ref):
    width = parts_r[0].shape[0]
    columns = []
    for real, imag in zip(parts_r, parts_i):
        high_r, low_r = split(real)
        high_i, low_i = split(imag)
        columns.append(jnp.concatenate([high_r, low_r, high_r, high_i, low_i, high_i], axis=0))
    data = jnp.concatenate(columns, axis=1)
    half = jnp.dot(left_ref[...], data, preferred_element_type=F32)
    rows = []
    for at in range(len(parts_r)):
        cut = slice(at * width, (at + 1) * width)
        high_r, low_r = split(half[:width, cut])
        high_i, low_i = split(half[width:, cut])
        rows.append(jnp.concatenate([high_r, low_r, high_r, high_i, low_i, high_i], axis=1))
    data = jnp.concatenate(rows, axis=0)
    whole = jnp.dot(data, right_ref[...], preferred_element_type=F32)
    out_r = [whole[at * width : (at + 1) * width, :width] for at in range(len(parts_r))]
    out_i = [whole[at * width : (at + 1) * width, width:] for at in range(len(parts_r))]
    return out_r, out_i


def neighbours():
    row, column = lax.axis_index("ty"), lax.axis_index("tx")
    has = {
        "up": row > 0,
        "down": row < lax.axis_size("ty") - 1,
        "left": column > 0,
        "right": column < lax.axis_size("tx") - 1,
    }
    where = {
        "up": {"ty": row - 1},
        "down": {"ty": row + 1},
        "left": {"tx": column - 1},
        "right": {"tx": column + 1},
    }
    return has, where


def greet(has, where):
    barrier = pltpu.get_barrier_semaphore()
    for side, there in has.items():

        @pl.when(there)
        def _():
            pl.semaphore_signal(
                barrier, inc=1, device_id=where[side], device_id_type=pl.DeviceIdType.MESH
            )

    peers = sum(there.astype(jnp.int32) for there in has.values())
    pl.semaphore_wait(barrier, peers)


class Link:
    def __init__(self, source, target, sems, at, device, sends, receives):
        self.copy = pltpu.make_async_remote_copy(
            src_ref=source,
            dst_ref=target,
            send_sem=sems[0].at[at],
            recv_sem=sems[1].at[at],
            device_id=device,
            device_id_type=pl.DeviceIdType.MESH,
        )
        self.sends, self.receives = sends, receives

    def start(self):
        pl.when(self.sends)(self.copy.start)

    def sent(self):
        pl.when(self.sends)(self.copy.wait_send)

    def arrived(self):
        pl.when(self.receives)(self.copy.wait_recv)


def window(region, plane, top, left):
    width = region.shape[-1] // 2
    base = pl.multiple_of(top // 8 * 8, 8)
    extra = top - base
    rows = region[plane, pl.ds(base, width + 8), :]
    back = jnp.where(left == 0, 0, 2 * width - left)
    rows = pltpu.roll(rows, back, 1)[:, :width]
    up = jnp.where(extra == 0, 0, width + 8 - extra)
    return pltpu.roll(rows, up, 0)[:width]


def deposit(totals, plane, value, top, left):
    width = value.shape[0]
    base = pl.multiple_of(top // 8 * 8, 8)
    tall = jnp.concatenate([value, jnp.zeros((8, width), F32)], axis=0)
    tall = pltpu.roll(tall, top - base, 0)
    wide = pltpu.roll(jnp.concatenate([tall, jnp.zeros_like(tall)], axis=1), left, 1)
    totals[plane, pl.ds(base, width + 8), :] += wide


def write_quarters(totals, upper_left, upper_right, lower_left, lower_right):
    width = upper_left.shape[-1]
    upper_left[...] = totals[:, :width, :width]
    upper_right[...] = totals[:, :width, width:]
    lower_left[...] = totals[:, width:, :width]
    lower_right[...] = totals[:, width:, width:]


class Halo:
    def __init__(self, own, region, sems, at, has, where):
        planes, width = own.shape[0], own.shape[-1]
        upper, lower = slice(0, width), slice(width, 2 * width)
        both = (has["up"] & has["right"], has["down"] & has["right"])
        self.own, self.region, self.has = own, region, has
        self.across, self.down, self.corner = [], [], []
        for plane in range(planes):
            mine = own.at[plane]
            right = region.at[plane, upper, lower]
            below = region.at[plane, lower, upper]
            beyond = region.at[plane, lower, lower]
            sem = at + 3 * plane
            self.across.append(
                Link(mine, right, sems, sem, where["left"], has["left"], has["right"])
            )
            self.down.append(
                Link(mine, below, sems, sem + 1, where["up"], has["up"], has["down"])
            )
            self.corner.append(Link(right, beyond, sems, sem + 2, where["up"], *both))

    def start(self):
        for link in (*self.across, *self.down):
            link.start()

    def blank(self):
        has, region, width = self.has, self.region, self.own.shape[-1]
        upper, lower = slice(0, width), slice(width, 2 * width)
        zeros = jnp.zeros(self.own.shape, F32)
        region[:, upper, upper] = self.own[...]

        @pl.when(jnp.logical_not(has["right"]))
        def _():
            region[:, upper, lower] = zeros

        @pl.when(jnp.logical_not(has["down"]))
        def _():
            region[:, lower, upper] = zeros

        @pl.when(jnp.logical_not(has["down"] & has["right"]))
        def _():
            region[:, lower, lower] = zeros

    def turn(self, plane):
        self.across[plane].arrived()
        self.corner[plane].start()

    def finish(self):
        for link in (*self.down, *self.corner):
            link.arrived()
        for link in (*self.across, *self.down, *self.corner):
            link.sent()


class Sums:
    def __init__(self, quarters, passing, got, sems, at, has, where):
        self.quarters, self.passing, self.got, self.has = quarters, passing, got, has
        _, _, lower_left, lower_right = quarters
        self.corner, self.down, self.across = [], [], []
        for plane in range(passing.shape[0]):
            sem = at + 3 * plane
            below = (where["down"], has["down"], has["up"])
            beside = (where["right"], has["right"], has["left"])
            self.corner.append(
                Link(lower_right.at[plane], got.at[0, plane], sems, sem, *below)
            )
            self.down.append(
                Link(lower_left.at[plane], got.at[1, plane], sems, sem + 1, *below)
            )
            self.across.append(Link(passing.at[plane], got.at[2, plane], sems, sem + 2, *beside))

    def start(self):
        for link in (*self.corner, *self.down):
            link.start()

    def blank(self):
        @pl.when(jnp.logical_not(self.has["up"]))
        def _():
            self.got[0:2] = jnp.zeros((2, *self.passing.shape), F32)

        @pl.when(jnp.logical_not(self.has["left"]))
        def _():
            self.got[2] = jnp.zeros(self.passing.shape, F32)

    def turn(self, plane):
        self.corner[plane].arrived()
        self.passing[plane] = self.quarters[1][plane] + self.got[0, plane]
        self.across[plane].start()

    def finish(self):
        for link in (*self.down, *self.across):
            link.arrived()
        for link in (*self.corner, *self.down, *self.across):
            link.sent()

    def total(self, plane):
        return self.quarters[0][plane] + self.got[1, plane] + self.got[2, plane]


def halo_kernel(own, region, *sems):
    has, where = neighbours()
    greet(has, where)
    halo = Halo(own, region, sems, 0, has, where)
    halo.start()
    halo.blank()
    for plane in range(own.shape[0]):
        halo.turn(plane)
    halo.finish()


def first_kernel(coords, live, region, probe, wave, *refs):
    *quarters, totals = refs
    totals[...] = jnp.zeros_like(totals)

    @pl.loop(0, coords.shape[0])
    def _(slot):
        top, left = coords[slot, 0], coords[slot, 1]
        real, imag = window(region, 0, top, left), window(region, 1, top, left)
        wave[slot, 0] = probe[0] * real - probe[1] * imag
        wave[slot, 1] = probe[0] * imag + probe[1] * real

        @pl.when(slot < live[0])
        def _():
            deposit(totals, 0, probe[0] * probe[0] + probe[1] * probe[1], top, left)

    write_quarters(totals, *quarters)


def double_transform(group, source, target, tables, between, after, hooks):
    steps = source.shape[0] // group

    @pl.loop(0, steps)
    def _(step):
        slots = [step * group + at for at in range(group)]
        spec_r, spec_i = forward(
            [source[slot, 0] for slot in slots], [source[slot, 1] for slot in slots], *tables
        )
        for at, hook in enumerate(hooks):
            if at % 2 == 0 and at // 2 < steps:
                pl.when(step == at // 2)(hook)
        moved = [between(slot, a, b) for slot, a, b in zip(slots, spec_r, spec_i)]
        out_r, minus_i = forward([m[0] for m in moved], [-m[1] for m in moved], *tables)
        for slot, a, b in zip(slots, out_r, minus_i):
            target[slot, 0], target[slot, 1] = after(a, -b)
        for at, hook in enumerate(hooks):
            if at % 2 == 1 and at // 2 < steps:
                pl.when(step == at // 2)(hook)

    for hook in hooks[2 * steps :]:
        hook()


def wave_kernel(group, source, own, n_ul, n_ur, n_ll, n_lr, phase, left_t, right_t, *refs):
    wave, region, norm_sum, passing, got, *sems = refs
    has, where = neighbours()
    greet(has, where)
    halo = Halo(own, region, sems, 0, has, where)
    sums = Sums((n_ul, n_ur, n_ll, n_lr), passing, got, sems, 3 * own.shape[0], has, where)
    halo.start()
    sums.start()
    halo.blank()
    sums.blank()

    def between(slot, real, imag):
        return real * phase[0] - imag * phase[1], real * phase[1] + imag * phase[0]

    hooks = [
        lambda: sums.turn(0),
        lambda: halo.turn(0),
        lambda: halo.turn(1),
    ]
    double_transform(
        group, source, wave, (left_t, right_t), between, lambda a, b: (a, b), hooks
    )
    halo.finish()
    sums.finish()
    norm_sum[...] = sums.total(0)


def second_kernel(coords, live, wave, region, exit_wave, patch, *refs):
    *quarters, totals = refs
    totals[...] = jnp.zeros_like(totals)

    @pl.loop(0, coords.shape[0])
    def _(slot):
        top, left = coords[slot, 0], coords[slot, 1]
        second_r, second_i = window(region, 0, top, left), window(region, 1, top, left)
        wave_r, wave_i = wave[slot, 0], wave[slot, 1]
        patch[slot, 0], patch[slot, 1] = second_r, second_i
        exit_wave[slot, 0] = wave_r * second_r - wave_i * second_i
        exit_wave[slot, 1] = wave_r * second_i + wave_i * second_r

        @pl.when(slot < live[0])
        def _():
            deposit(totals, 0, wave_r * wave_r + wave_i * wave_i, top, left)

    write_quarters(totals, *quarters)


def back_kernel(group, source, n_ul, n_ur, n_ll, n_lr, amplitude, left_t, right_t, *refs):
    back, norm_sum, passing, got, *sems = refs
    has, where = neighbours()
    greet(has, where)
    sums = Sums((n_ul, n_ur, n_ll, n_lr), passing, got, sems, 0, has, where)
    sums.start()
    sums.blank()

    def between(slot, real, imag):
        ratio = amplitude[slot] * jnp.minimum(lax.rsqrt(real * real + imag * imag), 2.0) - 1.0
        return real * ratio, imag * ratio

    double_transform(
        group,
        source,
        back,
        (left_t, right_t),
        between,
        lambda a, b: (a, b),
        [lambda: sums.turn(0)],
    )
    sums.finish()
    norm_sum[...] = sums.total(0)


def third_kernel(coords, live, wave, patch, back, inner, *refs):
    *quarters, totals = refs
    totals[...] = jnp.zeros_like(totals)

    @pl.loop(0, coords.shape[0])
    def _(slot):
        top, left = coords[slot, 0], coords[slot, 1]
        real, imag = back[slot, 0], back[slot, 1]
        second_r, second_i = patch[slot, 0], patch[slot, 1]
        inner[slot, 0] = second_r * real + second_i * imag
        inner[slot, 1] = second_r * imag - second_i * real

        @pl.when(slot < live[0])
        def _():
            wave_r, wave_i = wave[slot, 0], wave[slot, 1]
            deposit(totals, 0, wave_r * real + wave_i * imag, top, left)
            deposit(totals, 1, wave_r * imag - wave_i * real, top, left)

    write_quarters(totals, *quarters)


def grad_kernel(group, source, g_ul, g_ur, g_ll, g_lr, probe, phase, left_t, right_t, *refs):
    grad, grad_sum, passing, got, *sems = refs
    has, where = neighbours()
    greet(has, where)
    sums = Sums((g_ul, g_ur, g_ll, g_lr), passing, got, sems, 0, has, where)
    sums.start()
    sums.blank()

    def between(slot, real, imag):
        return real * phase[0] + imag * phase[1], imag * phase[0] - real * phase[1]

    def after(real, imag):
        return probe[0] * real + probe[1] * imag, probe[0] * imag - probe[1] * real

    double_transform(
        group,
        source,
        grad,
        (left_t, right_t),
        between,
        after,
        [lambda: sums.turn(0), lambda: sums.turn(1)],
    )
    sums.finish()
    for plane in range(2):
        grad_sum[plane] = sums.total(plane)


def fourth_kernel(coords, live, grad, *refs):
    *quarters, totals = refs
    totals[...] = jnp.zeros_like(totals)

    @pl.loop(0, live[0])
    def _(slot):
        top, left = coords[slot, 0], coords[slot, 1]
        deposit(totals, 0, grad[slot, 0], top, left)
        deposit(totals, 1, grad[slot, 1], top, left)

    write_quarters(totals, *quarters)


def last_kernel(g_ul, g_ur, g_ll, g_lr, *refs):
    grad_sum, passing, got, *sems = refs
    has, where = neighbours()
    greet(has, where)
    sums = Sums((g_ul, g_ur, g_ll, g_lr), passing, got, sems, 0, has, where)
    sums.start()
    sums.blank()
    for plane in range(2):
        sums.turn(plane)
    sums.finish()
    for plane in range(2):
        grad_sum[plane] = sums.total(plane)


def on_device(object_planes, probe, phase, coords, live, amplitude):
    width = probe.shape[-1]
    slots = coords.shape[2]
    group = 2 if slots % 2 == 0 else 1
    left_t, right_t = split_tables(width)
    phase_ri = jnp.stack([jnp.cos(phase), jnp.sin(phase)])
    place = (coords[0, 0], live[0])
    smem = pl.BlockSpec(memory_space=pltpu.SMEM)
    vmem = pl.BlockSpec(memory_space=pltpu.VMEM)

    def plane(*lead):
        return jax.ShapeDtypeStruct((*lead, width, width), F32)

    def double(planes):
        return jax.ShapeDtypeStruct((planes, 2 * width, 2 * width), F32)

    def totals(planes):
        return [pltpu.VMEM((planes, 2 * width, 2 * width), F32)]

    def wires(planes, links):
        sums = [pltpu.VMEM((planes, width, width), F32), pltpu.VMEM((3, planes, width, width), F32)]
        return (sums if planes else []) + [pltpu.SemaphoreType.DMA((links,))] * 2

    dots = 2 * slots * 2 * 2 * width * 2 * width * 6 * width

    def call(body, outs, scratches, name, scalars=0, ident=None, flops=1 << 20):
        def run(*args):
            return pl.pallas_call(
                body,
                out_shape=outs,
                in_specs=[smem] * scalars + [vmem] * (len(args) - scalars),
                out_specs=jax.tree.map(lambda _: vmem, outs),
                scratch_shapes=scratches,
                compiler_params=pltpu.CompilerParams(
                    vmem_limit_bytes=32 << 20,
                    collective_id=ident,
                    has_side_effects=ident is not None,
                ),
                cost_estimate=pl.CostEstimate(
                    flops=flops, bytes_accessed=8 << 20, transcendentals=0
                ),
                name=name,
            )(*args)

        return run

    def bind(body):
        def bound(*refs):
            body(group, *refs)

        return bound

    tables = (left_t, right_t)
    first, second = object_planes[0:2], object_planes[2:4]
    waves = plane(slots, 2)
    quarters = [plane(1)] * 4
    pairs = [plane(2)] * 4
    region_one = call(halo_kernel, double(2), wires(0, 6), "halo", ident=0)(first)
    incident, *norm_one = call(first_kernel, [waves, *quarters], totals(1), "first", 2)(
        *place, region_one, probe
    )
    wave, region_two, norm_one = call(
        bind(wave_kernel), [waves, double(2), plane()], wires(1, 9), "wave", ident=1, flops=dots
    )(incident, second, *norm_one, phase_ri, *tables)
    exit_wave, patch, *norm_two = call(
        second_kernel, [waves, waves, *quarters], totals(1), "second", 2
    )(*place, wave, region_two)
    back, norm_two = call(
        bind(back_kernel), [waves, plane()], wires(1, 3), "back", ident=2, flops=dots
    )(exit_wave, *norm_two, amplitude[0, 0], *tables)
    inner, *grad_two = call(third_kernel, [waves, *pairs], totals(2), "third", 2)(
        *place, wave, patch, back
    )
    grad, grad_two = call(
        bind(grad_kernel), [waves, plane(2)], wires(2, 6), "grad", ident=3, flops=dots
    )(inner, *grad_two, probe, phase_ri, *tables)
    grad_one = call(fourth_kernel, pairs, totals(2), "fourth", 2)(*place, grad)
    grad_one = call(last_kernel, plane(2), wires(2, 6), "last", ident=4)(*grad_one)
    new_first = first + grad_one / (norm_one + 1.0)
    new_second = second + grad_two / (norm_two + 1.0)
    return jnp.concatenate([new_first, new_second])


def solution(mesh):
    return jax.shard_map(
        on_device,
        mesh=mesh,
        in_specs=(
            P(None, ("groups", "ty"), "tx"),
            P(),
            P(),
            P(("groups", "ty"), "tx", None, None),
            P(("groups", "ty"), "tx"),
            P(("groups", "ty"), "tx", None, None, None),
        ),
        out_specs=P(None, ("groups", "ty"), "tx"),
        check_vma=False,
    )
```

```python
import math

import jax
import jax.numpy as jnp
import numpy as np
from jax import lax
from jax.experimental import pallas as pl
from jax.experimental.pallas import tpu as pltpu
from jax.sharding import PartitionSpec as P

F32 = jnp.float32
BF16 = jnp.bfloat16


def split_tables(width):
    index = np.arange(width)[:, None] * np.arange(width)[None, :] % width
    angles = index * (2.0 * math.pi / width)
    scale = 1.0 / math.sqrt(width)
    cos_table = (np.cos(angles) * scale).astype(np.float32)
    sin_table = (-np.sin(angles) * scale).astype(np.float32)

    def parts(table):
        high = table.astype(BF16)
        low = (table - high.astype(np.float32)).astype(BF16)
        return high, high, low

    left = np.concatenate(
        [
            np.concatenate([*parts(cos_table), *parts(-sin_table)], axis=1),
            np.concatenate([*parts(sin_table), *parts(cos_table)], axis=1),
        ],
        axis=0,
    )
    return jnp.asarray(left)


def split(value):
    high = value.astype(BF16)
    low = (value - high.astype(F32)).astype(BF16)
    return high, low


def forward(parts_r, parts_i, left_ref, right_ref):
    width = parts_r[0].shape[0]
    columns = []
    for real, imag in zip(parts_r, parts_i):
        high_r, low_r = split(real)
        high_i, low_i = split(imag)
        columns.append(jnp.concatenate([high_r, low_r, high_r, high_i, low_i, high_i], axis=0))
    data = jnp.concatenate(columns, axis=1)
    half = jnp.dot(left_ref[...], data, preferred_element_type=F32)
    rows = []
    for at in range(len(parts_r)):
        cut = slice(at * width, (at + 1) * width)
        high_r, low_r = split(half[:width, cut])
        high_i, low_i = split(half[width:, cut])
        rows.append(jnp.concatenate([high_r, low_r, high_r, high_i, low_i, high_i], axis=1))
    data = jnp.concatenate(rows, axis=0)
    whole = jnp.dot(data, right_ref[...], preferred_element_type=F32)
    out_r = [whole[at * width : (at + 1) * width, :width] for at in range(len(parts_r))]
    out_i = [whole[at * width : (at + 1) * width, width:] for at in range(len(parts_r))]
    return out_r, out_i


def neighbours():
    row, column = lax.axis_index("ty"), lax.axis_index("tx")
    has = {
        "up": row > 0,
        "down": row < lax.axis_size("ty") - 1,
        "left": column > 0,
        "right": column < lax.axis_size("tx") - 1,
    }
    where = {
        "up": {"ty": row - 1},
        "down": {"ty": row + 1},
        "left": {"tx": column - 1},
        "right": {"tx": column + 1},
    }
    return has, where


def greet(has, where):
    barrier = pltpu.get_barrier_semaphore()
    for side, there in has.items():

        @pl.when(there)
        def _():
            pl.semaphore_signal(
                barrier, inc=1, device_id=where[side], device_id_type=pl.DeviceIdType.MESH
            )

    peers = sum(there.astype(jnp.int32) for there in has.values())
    pl.semaphore_wait(barrier, peers)


class Link:
    def __init__(self, source, target, sems, at, device, sends, receives):
        self.copy = pltpu.make_async_remote_copy(
            src_ref=source,
            dst_ref=target,
            send_sem=sems[0].at[at],
            recv_sem=sems[1].at[at],
            device_id=device,
            device_id_type=pl.DeviceIdType.MESH,
        )
        self.sends, self.receives = sends, receives

    def start(self):
        pl.when(self.sends)(self.copy.start)

    def sent(self):
        pl.when(self.sends)(self.copy.wait_send)

    def arrived(self):
        pl.when(self.receives)(self.copy.wait_recv)


def window(region, plane, top, left):
    width = region.shape[-1] // 2
    base = pl.multiple_of(top // 8 * 8, 8)
    extra = top - base
    rows = region[plane, pl.ds(base, width + 8), :]
    back = jnp.where(left == 0, 0, 2 * width - left)
    rows = pltpu.roll(rows, back, 1)[:, :width]
    up = jnp.where(extra == 0, 0, width + 8 - extra)
    return pltpu.roll(rows, up, 0)[:width]


def deposit(totals, plane, value, top, left):
    width = value.shape[0]
    base = pl.multiple_of(top // 8 * 8, 8)
    tall = jnp.concatenate([value, jnp.zeros((8, width), F32)], axis=0)
    tall = pltpu.roll(tall, top - base, 0)
    wide = pltpu.roll(jnp.concatenate([tall, jnp.zeros_like(tall)], axis=1), left, 1)
    totals[plane, pl.ds(base, width + 8), :] += wide


def write_quarters(totals, upper_left, upper_right, lower_left, lower_right):
    width = upper_left.shape[-1]
    upper_left[...] = totals[:, :width, :width]
    upper_right[...] = totals[:, :width, width:]
    lower_left[...] = totals[:, width:, :width]
    lower_right[...] = totals[:, width:, width:]


class Halo:
    def __init__(self, own, region, sems, at, has, where):
        planes, width = own.shape[0], own.shape[-1]
        upper, lower = slice(0, width), slice(width, 2 * width)
        both = (has["up"] & has["right"], has["down"] & has["right"])
        self.own, self.region, self.has = own, region, has
        self.across, self.down, self.corner = [], [], []
        for plane in range(planes):
            mine = own.at[plane]
            right = region.at[plane, upper, lower]
            below = region.at[plane, lower, upper]
            beyond = region.at[plane, lower, lower]
            sem = at + 3 * plane
            self.across.append(
                Link(mine, right, sems, sem, where["left"], has["left"], has["right"])
            )
            self.down.append(
                Link(mine, below, sems, sem + 1, where["up"], has["up"], has["down"])
            )
            self.corner.append(Link(right, beyond, sems, sem + 2, where["up"], *both))

    def blank(self):
        has, region, width = self.has, self.region, self.own.shape[-1]
        upper, lower = slice(0, width), slice(width, 2 * width)
        zeros = jnp.zeros(self.own.shape, F32)
        region[:, upper, upper] = self.own[...]

        @pl.when(jnp.logical_not(has["right"]))
        def _():
            region[:, upper, lower] = zeros

        @pl.when(jnp.logical_not(has["down"]))
        def _():
            region[:, lower, upper] = zeros

        @pl.when(jnp.logical_not(has["down"] & has["right"]))
        def _():
            region[:, lower, lower] = zeros

    def turn(self, plane):
        self.across[plane].arrived()
        self.corner[plane].start()

    def finish(self, start):
        for link in (*self.down, *self.corner):
            link.arrived()
        for link in (*self.across[start:], *self.down, *self.corner):
            link.sent()


class Sums:
    def __init__(self, quarters, passing, got, sems, at, has, where):
        self.quarters, self.passing, self.got, self.has = quarters, passing, got, has
        _, _, lower_left, lower_right = quarters
        self.corner, self.down, self.across = [], [], []
        for plane in range(passing.shape[0]):
            sem = at + 3 * plane
            below = (where["down"], has["down"], has["up"])
            beside = (where["right"], has["right"], has["left"])
            self.corner.append(
                Link(lower_right.at[plane], got.at[0, plane], sems, sem, *below)
            )
            self.down.append(
                Link(lower_left.at[plane], got.at[1, plane], sems, sem + 1, *below)
            )
            self.across.append(Link(passing.at[plane], got.at[2, plane], sems, sem + 2, *beside))

    def start(self):
        self.corner[0].start()

    def blank(self):
        @pl.when(jnp.logical_not(self.has["up"]))
        def _():
            self.got[0:2] = jnp.zeros((2, *self.passing.shape), F32)

        @pl.when(jnp.logical_not(self.has["left"]))
        def _():
            self.got[2] = jnp.zeros(self.passing.shape, F32)

    def turn(self, plane):
        self.corner[plane].arrived()
        for link in self.corner[plane + 1 : plane + 2] or self.down:
            link.start()
        self.passing[plane] = self.quarters[1][plane] + self.got[0, plane]
        self.across[plane].start()

    def finish(self):
        for link in (*self.down, *self.across):
            link.arrived()
        for link in (*self.corner, *self.down, *self.across):
            link.sent()

    def total(self, plane):
        return self.quarters[0][plane] + self.got[1, plane] + self.got[2, plane]


def turn_of(phase):
    half = phase * 0.5
    square = half * half
    for at in range(7, -1, -1):
        sign = -1.0 if at % 2 else 1.0
        if at == 7:
            cosine, sine = sign * (1.0 / math.factorial(14)), sign * (1.0 / math.factorial(15))
        else:
            cosine = cosine * square + sign / math.factorial(2 * at)
            sine = sine * square + sign / math.factorial(2 * at + 1)
    sine = sine * half
    return 1.0 - 2.0 * sine * sine, 2.0 * sine * cosine


def cut(parts, top, left):
    tall, wide = parts.shape[0], parts.shape[0]
    width = tall // 2
    row = lax.broadcasted_iota(jnp.int32, (width, tall), 0)
    column = lax.broadcasted_iota(jnp.int32, (width, tall), 1)
    pick = jnp.where(column - row == top, 1.0, 0.0).astype(BF16)
    rows = jnp.dot(pick, parts[...], preferred_element_type=F32).astype(BF16)
    rows = jnp.concatenate([rows[:, : 2 * wide], rows[:, 2 * wide :]], axis=0)
    row = lax.broadcasted_iota(jnp.int32, (wide, width), 0)
    column = lax.broadcasted_iota(jnp.int32, (wide, width), 1)
    pick = jnp.where(row - column == left, 1.0, 0.0).astype(BF16)
    both = jnp.dot(rows, jnp.concatenate([pick, pick], axis=0), preferred_element_type=F32)
    return both[:width], both[width:]


def double_transform(group, count, source, target, tables, between, after, hooks):
    steps = count // group

    @pl.loop(0, steps)
    def _(step):
        slots = [step * group + at for at in range(group)]
        inputs = [source(slot) for slot in slots]
        spec_r, spec_i = forward([a for a, _ in inputs], [b for _, b in inputs], *tables)
        for at, hook in enumerate(hooks):
            if at % 2 == 0 and at // 2 < steps:
                pl.when(step == at // 2)(hook)
        moved = [between(slot, a, b) for slot, a, b in zip(slots, spec_r, spec_i)]
        out_r, minus_i = forward([m[0] for m in moved], [-m[1] for m in moved], *tables)
        for slot, a, b in zip(slots, out_r, minus_i):
            target[slot, 0], target[slot, 1] = after(a, -b)
        for at, hook in enumerate(hooks):
            if at % 2 == 1 and at // 2 < steps:
                pl.when(step == at // 2)(hook)

    for hook in hooks[2 * steps :]:
        hook()


def wave_kernel(group, coords, own, probe, phase, left_t, *refs):
    wave, region_two, right_t, phase_ri, region_one, parts, *sems = refs
    width = own.shape[-1]
    has, where = neighbours()
    greet(has, where)
    one = Halo(own.at[0:2], region_one, sems, 0, has, where)
    two = Halo(own.at[2:4], region_two, sems, 6, has, where)
    one.across[0].start()
    one.down[0].start()
    one.down[1].start()
    one.blank()
    two.blank()
    for at in range(6):
        rows = slice(at * width, (at + 1) * width)
        right_t[rows, :width] = left_t[:width, rows]
        right_t[rows, width:] = left_t[width:, rows]
    phase_ri[0], phase_ri[1] = turn_of(phase[...])
    one.across[0].sent()
    one.across[1].start()
    one.turn(0)
    one.across[1].sent()
    two.across[0].start()
    one.turn(1)
    one.finish(start=2)
    tall = 2 * width
    for plane in range(2):
        high, low = split(region_one[plane])
        parts[:, 2 * plane * tall : (2 * plane + 1) * tall] = high
        parts[:, (2 * plane + 1) * tall : (2 * plane + 2) * tall] = low

    def source(slot):
        real, imag = cut(parts, coords[slot, 0], coords[slot, 1])
        return probe[0] * real - probe[1] * imag, probe[0] * imag + probe[1] * real

    def between(slot, real, imag):
        return (
            real * phase_ri[0] - imag * phase_ri[1],
            real * phase_ri[1] + imag * phase_ri[0],
        )

    def second_part():
        two.across[0].sent()
        two.across[1].start()
        two.down[0].start()
        two.down[1].start()

    hooks = [second_part, lambda: two.turn(0), lambda: two.turn(1)]
    count = coords.shape[0]
    double_transform(
        group, count, source, wave, (left_t, right_t), between, lambda a, b: (a, b), hooks
    )
    two.finish(start=1)


def second_kernel(coords, live, probe, wave, region, exit_wave, patch, *refs):
    *quarters, totals = refs
    totals[...] = jnp.zeros_like(totals)

    @pl.loop(0, coords.shape[0])
    def _(slot):
        top, left = coords[slot, 0], coords[slot, 1]
        second_r, second_i = window(region, 0, top, left), window(region, 1, top, left)
        wave_r, wave_i = wave[slot, 0], wave[slot, 1]
        patch[slot, 0], patch[slot, 1] = second_r, second_i
        exit_wave[slot, 0] = wave_r * second_r - wave_i * second_i
        exit_wave[slot, 1] = wave_r * second_i + wave_i * second_r

        @pl.when(slot < live[0])
        def _():
            deposit(totals, 0, probe[0] * probe[0] + probe[1] * probe[1], top, left)
            deposit(totals, 1, wave_r * wave_r + wave_i * wave_i, top, left)

    write_quarters(totals, *quarters)


def back_kernel(group, source, n_ul, n_ur, n_ll, n_lr, amplitude, left_t, right_t, *refs):
    back, norm_sum, passing, got, *sems = refs
    has, where = neighbours()
    greet(has, where)
    sums = Sums((n_ul, n_ur, n_ll, n_lr), passing, got, sems, 0, has, where)
    sums.start()
    sums.blank()

    def between(slot, real, imag):
        ratio = amplitude[slot] * jnp.minimum(lax.rsqrt(real * real + imag * imag), 2.0) - 1.0
        return real * ratio, imag * ratio

    double_transform(
        group,
        source.shape[0],
        lambda slot: (source[slot, 0], source[slot, 1]),
        back,
        (left_t, right_t),
        between,
        lambda a, b: (a, b),
        [lambda: sums.turn(0), lambda: sums.turn(1)],
    )
    sums.finish()
    for plane in range(2):
        norm_sum[plane] = sums.total(plane)


def third_kernel(coords, live, wave, patch, back, inner, *refs):
    *quarters, totals = refs
    totals[...] = jnp.zeros_like(totals)

    @pl.loop(0, coords.shape[0])
    def _(slot):
        top, left = coords[slot, 0], coords[slot, 1]
        real, imag = back[slot, 0], back[slot, 1]
        second_r, second_i = patch[slot, 0], patch[slot, 1]
        inner[slot, 0] = second_r * real + second_i * imag
        inner[slot, 1] = second_r * imag - second_i * real

        @pl.when(slot < live[0])
        def _():
            wave_r, wave_i = wave[slot, 0], wave[slot, 1]
            deposit(totals, 0, wave_r * real + wave_i * imag, top, left)
            deposit(totals, 1, wave_r * imag - wave_i * real, top, left)

    write_quarters(totals, *quarters)


def grad_kernel(group, source, g_ul, g_ur, g_ll, g_lr, probe, phase, left_t, right_t, *refs):
    grad, grad_sum, passing, got, *sems = refs
    has, where = neighbours()
    greet(has, where)
    sums = Sums((g_ul, g_ur, g_ll, g_lr), passing, got, sems, 0, has, where)
    sums.start()
    sums.blank()

    def between(slot, real, imag):
        return real * phase[0] + imag * phase[1], imag * phase[0] - real * phase[1]

    def after(real, imag):
        return probe[0] * real + probe[1] * imag, probe[0] * imag - probe[1] * real

    double_transform(
        group,
        source.shape[0],
        lambda slot: (source[slot, 0], source[slot, 1]),
        grad,
        (left_t, right_t),
        between,
        after,
        [lambda: sums.turn(0), lambda: sums.turn(1)],
    )
    sums.finish()
    for plane in range(2):
        grad_sum[plane] = sums.total(plane)


def fourth_kernel(coords, live, grad, *refs):
    *quarters, totals = refs
    totals[...] = jnp.zeros_like(totals)

    @pl.loop(0, live[0])
    def _(slot):
        top, left = coords[slot, 0], coords[slot, 1]
        deposit(totals, 0, grad[slot, 0], top, left)
        deposit(totals, 1, grad[slot, 1], top, left)

    write_quarters(totals, *quarters)


def last_kernel(g_ul, g_ur, g_ll, g_lr, *refs):
    grad_sum, passing, got, *sems = refs
    has, where = neighbours()
    greet(has, where)
    sums = Sums((g_ul, g_ur, g_ll, g_lr), passing, got, sems, 0, has, where)
    sums.start()
    sums.blank()
    for plane in range(g_ul.shape[0]):
        sums.turn(plane)
    sums.finish()
    for plane in range(g_ul.shape[0]):
        grad_sum[plane] = sums.total(plane)


def on_device(object_planes, probe, phase, coords, live, amplitude):
    width = probe.shape[-1]
    slots = coords.shape[2]
    group = 2 if slots % 2 == 0 else 1
    left_t = split_tables(width)
    place = (coords[0, 0], live[0])
    smem = pl.BlockSpec(memory_space=pltpu.SMEM)
    vmem = pl.BlockSpec(memory_space=pltpu.VMEM)

    def plane(*lead):
        return jax.ShapeDtypeStruct((*lead, width, width), F32)

    def double(planes):
        return jax.ShapeDtypeStruct((planes, 2 * width, 2 * width), F32)

    def totals(planes):
        return [pltpu.VMEM((planes, 2 * width, 2 * width), F32)]

    def wires(lead, rows, links):
        return [
            pltpu.VMEM((lead, rows, width), F32),
            pltpu.VMEM((3, lead, rows, width), F32),
            pltpu.SemaphoreType.DMA((links,)),
            pltpu.SemaphoreType.DMA((links,)),
        ]

    dots = 2 * slots * 2 * 2 * width * 2 * width * 6 * width

    def call(body, outs, scratches, name, scalars=0, ident=None, flops=1 << 20):
        def run(*args):
            return pl.pallas_call(
                body,
                out_shape=outs,
                in_specs=[smem] * scalars + [vmem] * (len(args) - scalars),
                out_specs=jax.tree.map(lambda _: vmem, outs),
                scratch_shapes=scratches,
                compiler_params=pltpu.CompilerParams(
                    vmem_limit_bytes=32 << 20,
                    collective_id=ident,
                    has_side_effects=ident is not None,
                ),
                cost_estimate=pl.CostEstimate(
                    flops=flops, bytes_accessed=8 << 20, transcendentals=0
                ),
                name=name,
            )(*args)

        return run

    def bind(body):
        def bound(*refs):
            body(group, *refs)

        return bound

    first, second = object_planes[0:2], object_planes[2:4]
    waves = plane(slots, 2)
    pairs = [plane(2)] * 4
    turned = jax.ShapeDtypeStruct((6 * width, 2 * width), BF16)
    wave, region_two, right_t, phase_ri = call(
        bind(wave_kernel),
        [waves, double(2), turned, plane(2)],
        [
            *totals(2),
            pltpu.VMEM((2 * width, 8 * width), BF16),
            pltpu.SemaphoreType.DMA((12,)),
            pltpu.SemaphoreType.DMA((12,)),
        ],
        "wave",
        1,
        ident=0,
        flops=dots,
    )(place[0], object_planes, probe, phase, left_t)
    tables = (left_t, right_t)
    exit_wave, patch, *norms = call(
        second_kernel, [waves, waves, *pairs], totals(2), "second", 2
    )(*place, probe, wave, region_two)
    back, norms = call(
        bind(back_kernel), [waves, plane(2)], wires(2, width, 6), "back", ident=1, flops=dots
    )(exit_wave, *norms, amplitude[0, 0], *tables)
    inner, *grad_two = call(third_kernel, [waves, *pairs], totals(2), "third", 2)(
        *place, wave, patch, back
    )
    grad, grad_two = call(
        bind(grad_kernel), [waves, plane(2)], wires(2, width, 6), "grad", ident=2, flops=dots
    )(inner, *grad_two, probe, phase_ri, *tables)
    grad_one = call(fourth_kernel, pairs, totals(2), "fourth", 2)(*place, grad)
    halves = (4, width // 2, width)
    grad_one = call(
        last_kernel,
        jax.ShapeDtypeStruct(halves, F32),
        wires(4, width // 2, 12),
        "last",
        ident=3,
    )(*[quarter.reshape(halves) for quarter in grad_one]).reshape(2, width, width)
    new_first = first + grad_one / (norms[0:1] + 1.0)
    new_second = second + grad_two / (norms[1:2] + 1.0)
    return jnp.concatenate([new_first, new_second])


def solution(mesh):
    return jax.shard_map(
        on_device,
        mesh=mesh,
        in_specs=(
            P(None, ("groups", "ty"), "tx"),
            P(),
            P(),
            P(("groups", "ty"), "tx", None, None),
            P(("groups", "ty"), "tx"),
            P(("groups", "ty"), "tx", None, None, None),
        ),
        out_specs=P(None, ("groups", "ty"), "tx"),
        check_vma=False,
    )
```
